1024 devices in a mesh: group: 64 (over z_hi, y, core), head: 16 (over z_lo, x).
Axes of the slice: x: 8, y: 8, z: 8 (z_hi: 4, z_lo: 2; z = z_hi * 2 + z_lo), core: 2. Of those that a mesh axis runs over, the one named last changes fastest.
Arguments:
- key_grad: bfloat16 [32768, 16384], P('group', 'head'), may hold values from -16 to 16
- value_grad: bfloat16 [32768, 16384], P('group', 'head'), may hold values from -6 to 6
- rope_grad: bfloat16 [32768, 8192], P('group', 'head'), may hold values from -1.5 to 1.5
- key_lift: bfloat16 [512, 16384], P(None, 'head'), may hold values from -0.046875 to 0.046875
- value_lift: bfloat16 [512, 16384], P(None, 'head'), may hold values from -0.046875 to 0.046875
- latent: bfloat16 [32768, 512], P('group'), may hold values from -40 to 40
- norm_gain: float32 [512], replicated, may hold values from 0.25 to 1.75
- doc_lengths: int32 [64, 4], P('group'), may hold values from 1 to 256, 512 in all within a row
- hidden: bfloat16 [32768, 7168], P('group', 'head'), may hold values from -0.078125 to 0.078125
- down_proj: bfloat16 [7168, 576], P('head'), may hold values from -0.0625 to 0.0625
Outputs:
- hidden_grad: bfloat16 [32768, 7168], P('group', 'head')
- weight_grad: float32 [576, 7168], P('group', 'head')
The draws below stay inside these ranges and needn't reach their ends.
Inputs may be any that keep to these rules, and one draw needn't show every extreme that they name: `doc_lengths`: each row sums to 512 and its largest entry is 256.
All inputs are finite; a program needn't handle non-finite values.
Results may differ from the reference program's by a relative error of at most 0.0049.
Values may be sent and summed in bfloat16 or wider, within the bound.
A program may use at most 32 MiB of HBM per device.

```python
import math
import jax
import jax.numpy as jnp
import numpy as np
from jax import lax

D = 7168
HEADS = 128
HD = 128
VD = 128
LATENT = 512
ROPE = 64
SEQ = 512
DOCS = 4
KVW = 576
TOKENS = 32768
MOST_DOC = 256
N_GROUP = 64


def draw_latent(key, part):
    first_key, second_key = jax.random.split(key, 2)
    row_scale = jnp.exp(jax.random.uniform(second_key, (TOKENS, 1), jnp.float32, 0.0, math.log(10.0)))
    base = jnp.clip(jax.random.normal(first_key, (TOKENS, LATENT), jnp.float32), -4.0, 4.0)
    values = base * row_scale
    return values.astype(jnp.bfloat16)


def spiked(result, key, source, target, parts, factor):
    def block_of(dim):
        return (jnp.arange(result.shape[dim]) // (result.shape[dim] // parts)).reshape((-1,) + (1,) * (result.ndim - 1 - dim))

    first = jax.random.permutation(key, parts)[block_of(target)]
    other_side = (block_of(target) + parts // 2) % parts
    return jnp.where((block_of(source) == first) | (block_of(source) == other_side), factor * result, result)


def level_of(stream_key, dims, cuts, smallest, high):
    gain, own = 1.0, jax.random.fold_in(stream_key, 6)
    for dim, shards_of in cuts:
        steps = jnp.exp(jax.random.uniform(jax.random.fold_in(own, dim), (shards_of,), jnp.float32, smallest / len(cuts), high / len(cuts)))
        gain = gain * jnp.repeat(steps, dims[dim] // shards_of).reshape([-1 if axis == dim else 1 for axis in range(len(dims))])
    return gain


def split_up(amount, total, limit, lean):
    loads = [(1 << 20) // math.isqrt(rank ** lean) + 1 for rank in range(2, amount + 1)]
    rest, given = total - limit - (amount - 1), [1] * (amount - 1)
    while rest > 0:
        movable = [i for i in range(amount - 1) if given[i] < limit]
        whole, budget = sum([loads[i] for i in movable]), rest
        for i in movable:
            addition = min(limit - given[i], max(1, budget * loads[i] // whole), rest)
            given[i] = given[i] + addition
            rest = rest - addition
    return np.array([limit] + given)


def uneven_parts(own_key, count, total, limit, skew):
    if count == 2:
        one = jax.random.randint(own_key, (), max(1, total - limit), min(limit, total - 1) + 1)
        return jnp.stack([one, total - one])
    sizes = jnp.asarray(split_up(count, total, limit, skew), jnp.int32)
    pairs = (count - 1) // 2
    source_of, taker = sizes[1:1 + 2 * pairs:2], sizes[2:2 + 2 * pairs:2]
    slack = jnp.minimum(source_of - 1, limit - taker)
    passed = jax.random.randint(jax.random.fold_in(own_key, 1), (pairs,), 0, 1 << 20) % (slack + 1)
    sizes = sizes.at[1:1 + 2 * pairs:2].set(source_of - passed).at[2:2 + 2 * pairs:2].set(taker + passed)
    return sizes[jax.random.permutation(jax.random.fold_in(own_key, 2), count)]


def centred(rng, shape, scale, limit, pieces=(), kind=jnp.bfloat16):
    result = jax.random.normal(rng, shape, jnp.float32) * scale
    if len(pieces) > 0:
        result = level_of(rng, shape, pieces, -0.22, 0.18) * result
    return jnp.clip(result, min=-limit, max=limit).astype(kind)


def heavy_noise(stream_key, dims, spread, reach, cuts, heavy, kind=jnp.bfloat16):
    entries = spread * jax.random.normal(stream_key, dims, jnp.float32)
    if cuts:
        entries = entries * level_of(stream_key, dims, cuts, -0.22, 0.18)
    return jnp.clip(spiked(entries, jax.random.fold_in(stream_key, 3), *heavy), -reach, reach).astype(kind)


def setup_inputs(seed: int = 0) -> dict:
    splits = jax.random.split(jax.random.key(seed), 11)
    key_grad = heavy_noise(splits[0], (TOKENS, HEADS * HD), 1.0, 16.0, ((0, 64), (1, 16)), (1, 0, 64, 4.0))
    value_grad = centred(splits[1], (TOKENS, HEADS * VD), 1.0, 6.0, ((0, 64), (1, 16)))
    rope_grad = centred(splits[2], (TOKENS, HEADS * ROPE), 0.1, 1.5, ((0, 64), (1, 16)))
    key_lift = centred(splits[3], (LATENT, HEADS * HD), (HEADS * HD) ** -0.5, 0.046875, ((1, 16),))
    value_lift = centred(splits[4], (LATENT, HEADS * VD), (HEADS * VD) ** -0.5, 0.046875, ((1, 16),))
    latent = draw_latent(jax.random.fold_in(splits[10], 71), 0)
    norm_gain = jnp.clip(1.0 + 0.15 * jax.random.normal(splits[6], (LATENT,), jnp.float32), 0.25, 1.75)
    doc_lengths = jax.vmap(lambda own: uneven_parts(own, DOCS, SEQ, MOST_DOC, 2))(jax.random.split(splits[7], N_GROUP)).reshape((N_GROUP, DOCS)).astype(jnp.int32)
    hidden = centred(splits[8], (TOKENS, D), (TOKENS ** -0.5), 0.078125, ((0, 64), (1, 16)))
    down_proj = centred(splits[9], (D, KVW), D ** -0.5, 0.0625, ((0, 16),))
    return {"key_grad": key_grad, "value_grad": value_grad, "rope_grad": rope_grad, "key_lift": key_lift, "value_lift": value_lift, "latent": latent, "norm_gain": norm_gain, "doc_lengths": doc_lengths, "hidden": hidden, "down_proj": down_proj}


def positions(lengths, token_index):
    doc_ends = jnp.cumsum(lengths, axis=1).astype(jnp.int32)
    doc_start = lax.optimization_barrier(jnp.max(jnp.where(doc_ends <= token_index[:, None], doc_ends, 0), axis=1))
    return (token_index - doc_start).astype(jnp.int32)

def kva_rows_grad(stacked, latent, norm_gain, position):
    latent_part = stacked[:, :LATENT]
    rotary_part = stacked[:, LATENT:]
    values = latent.astype(jnp.float32)
    inverse_rms = lax.rsqrt(lax.optimization_barrier(jnp.mean(values * values, axis=1, keepdims=True)) + 1e-06)
    scaled_grad = latent_part * norm_gain[None, :]
    norm_grad = inverse_rms * (scaled_grad - values * inverse_rms * inverse_rms * lax.optimization_barrier(jnp.mean(scaled_grad * values, axis=1, keepdims=True)))
    half_width = rotary_part.shape[1] // 2
    inv_freq = 10000.0 ** (-(2.0 * jnp.arange(half_width, dtype=jnp.float32)) / (2.0 * half_width))
    angles = position.astype(jnp.float32)[:, None] * inv_freq[None, :]
    cosine = jnp.cos(angles)
    sine = jnp.sin(angles)
    first_half = rotary_part[:, :half_width]
    second_half = rotary_part[:, half_width:]
    rot_first = first_half * cosine + second_half * sine
    rot_second = second_half * cosine - first_half * sine
    return jnp.concatenate([norm_grad, rot_first, rot_second], axis=1).astype(jnp.bfloat16)

def reference(key_grad, value_grad, rope_grad, key_lift, value_lift, latent, norm_gain, doc_lengths, hidden, down_proj):
    latent_sum = jnp.dot(key_grad, key_lift.T, preferred_element_type=jnp.float32)
    latent_sum = latent_sum + jnp.dot(value_grad, value_lift.T, preferred_element_type=jnp.float32)
    tokens_all = key_grad.shape[0]
    rope_sum = lax.optimization_barrier(jnp.sum(rope_grad.reshape(tokens_all, HEADS, ROPE), axis=1, dtype=jnp.float32))
    stacked = jnp.concatenate([latent_sum, rope_sum], axis=1)
    token_ids = jnp.arange(tokens_all, dtype=jnp.int32)
    row_lengths = doc_lengths[(token_ids // SEQ).astype(jnp.int32)]
    position = positions(row_lengths, (token_ids % SEQ).astype(jnp.int32))
    kva_grad = kva_rows_grad(stacked, latent, norm_gain, position)
    hidden_grad = jnp.dot(kva_grad, down_proj.T, preferred_element_type=jnp.float32).astype(jnp.bfloat16)
    weight_grad = jnp.dot(kva_grad.T, hidden, preferred_element_type=jnp.float32)
    return (hidden_grad, weight_grad)
```

```python
import functools

import jax
import jax.numpy as jnp
from jax import lax
from jax.experimental import pallas as pl
from jax.experimental.pallas import tpu as pltpu
from jax.sharding import PartitionSpec as P

LATENT = 512
ROPE = 64
KVW = LATENT + ROPE
ROWS = 32
TILES = KVW * ROWS // (16 * 128)
MESH = pl.DeviceIdType.MESH
NT = (((1,), (1,)), ((), ()))
TT = (((0,), (1,)), ((), ()))
NN = (((1,), (0,)), ((), ()))
F32 = jnp.float32
BF16 = jnp.bfloat16


class Layout:
    def __init__(self, nzh, ny, nx):
        self.nzh, self.ny, self.nx = nzh, ny, nx
        self.heads = 2 * nx
        self.groups = 2 * ny * nzh
        self.seq = ROWS * self.heads
        self.own = KVW // self.groups
        self.block = -(-nzh * self.own // 8) * 8
        self.used = 2 * ny * self.block
        self.kp = -(-self.used // 128) * 128
        self.ownp = -(-self.own // 16) * 16


def far_first(n):
    return sorted(range(1, n), key=lambda d: (-min(d, n - d), d))


def dot(a, b, dims):
    return lax.dot_general(a, b, dims, preferred_element_type=F32)


def kernel(
    lay,
    key_hbm,
    value_hbm,
    rope_hbm,
    key_lift_hbm,
    value_lift_hbm,
    latent_hbm,
    gain_hbm,
    docs_hbm,
    hidden_hbm,
    down_hbm,
    hidden_out,
    weight_out,
    key_v,
    value_v,
    rope_v,
    key_lift_v,
    value_lift_v,
    latent_v,
    gain_v,
    docs_s,
    hidden_v,
    down_v,
    load_sem,
    fold_v,
    pick_v,
    down_p,
    own_a,
    zsend,
    zrecv,
    xsend,
    xrecv,
    acc_a,
    sum_a,
    kv_row,
    kva,
    w_f32,
    csend,
    crecv,
    ysend,
    yrecv,
    acc_c,
    hi_f32,
    hi_send,
    hi_recv,
    hid_v,
    out_sem,
    zs_sem,
    zr_sem,
    xs_sem,
    xr_sem,
    gs_sem,
    gr_sem,
    fs_sem,
    fr_sem,
    cs_sem,
    cr_sem,
    ys_sem,
    yr_sem,
    hs_sem,
    hr_sem,
):
    nx, ny, nzh = lay.nx, lay.ny, lay.nzh
    half = lay.seq // 2
    g = lax.axis_index("group")
    h = lax.axis_index("head")
    core, y, zh = g % 2, (g // 2) % ny, g // (2 * ny)
    x, zl = h % nx, h // nx

    z_peer = (g, (1 - zl) * nx + x)
    core_peer = (g + 1 - 2 * core, h)
    x_peer = {d: (g, zl * nx + (x + d) % nx) for d in range(1, nx)}
    y_peer = {d: ((zh * ny + (y + d) % ny) * 2 + core, h) for d in range(1, ny)}
    h_peer = {d: ((((zh + d) % nzh) * ny + y) * 2 + core, h) for d in range(1, nzh)}
    peers = [z_peer, core_peer, *x_peer.values(), *y_peer.values(), *h_peer.values()]

    barrier = pltpu.get_barrier_semaphore()
    for peer in peers:
        pl.semaphore_signal(barrier, inc=1, device_id=peer, device_id_type=MESH)

    theirs = pl.ds(pl.multiple_of((1 - zl) * half, half), half)
    mine = pl.ds(pl.multiple_of(zl * half, half), half)
    own_rows = pl.ds(pl.multiple_of(h * ROWS, ROWS), ROWS)
    loads = []

    def load(src, dst):
        copy = pltpu.make_async_copy(src, dst, load_sem.at[len(loads)])
        copy.start()
        loads.append(copy)
        return copy

    first = [
        load(key_lift_hbm, key_lift_v),
        load(key_hbm.at[theirs, :], key_v.at[0]),
        load(value_lift_hbm, value_lift_v),
        load(value_hbm.at[theirs, :], value_v.at[0]),
        load(rope_hbm.at[theirs, :], rope_v.at[0]),
    ]
    second = [
        load(key_hbm.at[mine, :], key_v.at[1]),
        load(value_hbm.at[mine, :], value_v.at[1]),
        load(rope_hbm.at[mine, :], rope_v.at[1]),
    ]
    third = [
        load(down_hbm, down_v),
        load(latent_hbm.at[own_rows, :], latent_v),
        load(gain_hbm, gain_v),
        load(docs_hbm, docs_s),
        load(hidden_hbm, hidden_v),
    ]

    width = rope_v.shape[2]
    fold_row = lax.broadcasted_iota(jnp.int32, (width, 128), 0)
    fold_col = lax.broadcasted_iota(jnp.int32, (width, 128), 1)
    fold_v[...] = jnp.where((fold_row & 63) == (fold_col & 63), 1.0, 0.0).astype(BF16)
    low = lax.broadcasted_iota(jnp.int32, (16, 128), 1) < 64

    def partial(part):
        terms = dot(key_v[part], key_lift_v[...], NT) + dot(value_v[part], value_lift_v[...], NT)
        return terms, dot(rope_v[part], fold_v[...], NN)

    def tiles(terms, ropes, chunk):
        base = chunk * ROWS
        for block in range(2):
            rows = slice(base + 16 * block, base + 16 * block + 16)
            for lane in range(4):
                yield 4 * block + lane, terms[rows, 128 * lane : 128 * lane + 128]
        yield 8, jnp.where(low, ropes[base : base + 16], ropes[base + 16 : base + 32])

    for copy in first:
        copy.wait()
    terms, ropes = partial(0)
    for chunk in range(nx):
        for i, tile in tiles(terms, ropes, chunk):
            zsend[chunk, i] = tile.astype(BF16)
    pl.semaphore_wait(barrier, len(peers))

    order = far_first(nx) + [0]
    z_copies = {}
    for d in order:
        to = (x + d) % nx
        z_copies[d] = pltpu.make_async_remote_copy(
            zsend.at[to], zrecv.at[to], zs_sem.at[d], zr_sem.at[d], device_id=z_peer, device_id_type=MESH
        )
        z_copies[d].start()
    for copy in second:
        copy.wait()
    terms, ropes = partial(1)
    for chunk in range(nx):
        for i, tile in tiles(terms, ropes, chunk):
            own_a[chunk, i] = tile

    x_copies = {}
    for d in order:
        to = (x + d) % nx
        z_copies[d].wait_recv()
        total = own_a[to] + zrecv[to].astype(F32)
        if d == 0:
            acc_a[...] = total
        else:
            xsend[d] = total.astype(BF16)
            x_copies[d] = pltpu.make_async_remote_copy(
                xsend.at[d], xrecv.at[d], xs_sem.at[d], xr_sem.at[d], device_id=x_peer[d], device_id_type=MESH
            )
            x_copies[d].start()

    for copy in third:
        copy.wait()
    block, own = lay.block, lay.own
    col = lax.broadcasted_iota(jnp.int32, (KVW, lay.kp), 1)
    row = lax.broadcasted_iota(jnp.int32, (KVW, lay.kp), 0)
    chunk_of = jnp.zeros_like(col)
    for k in range(1, 2 * ny):
        chunk_of = chunk_of + jnp.where(col >= k * block, 1, 0)
    q = col - chunk_of * block
    hi_of = jnp.zeros_like(col)
    for k in range(1, nzh):
        hi_of = hi_of + jnp.where(q >= k * own, 1, 0)
    core_of = jnp.where(chunk_of >= ny, 1, 0)
    source = ((hi_of * ny + chunk_of - core_of * ny) * 2 + core_of) * own + q - hi_of * own
    picked = (row == source) & (q < nzh * own) & (col < lay.used)
    pick_v[...] = jnp.where(picked, 1.0, 0.0).astype(BF16)
    down_p[...] = dot(down_v[...], pick_v[...], NN).astype(BF16)

    lane = lax.broadcasted_iota(jnp.int32, (16, 128), 1)
    token = h * ROWS + lax.broadcasted_iota(jnp.int32, (16, 128), 0) + jnp.where(low, 0, 16)
    start = jnp.zeros_like(token)
    end = jnp.int32(0)
    for k in range(docs_s.shape[1]):
        end = end + docs_s[0, k]
        start = jnp.maximum(start, jnp.where(token >= end, end, 0))
    position = (token - start).astype(F32)
    pair = (lane & 31).astype(F32)
    angle = position * jnp.exp(pair * (-2.0 / ROPE * 9.210340371976184))
    cosine, sine = jnp.cos(angle), jnp.sin(angle)
    front = (lane & 32) == 0
    sine = jnp.where(front, sine, -sine)
    values = latent_v[...].astype(F32)
    inverse = lax.rsqrt(jnp.mean(values * values, axis=1, keepdims=True) + 1e-06)

    for d in far_first(nx):
        x_copies[d].wait_recv()
        acc_a[...] += xrecv[d].astype(F32)

    for rb in range(2):
        for lb in range(4):
            sum_a[16 * rb : 16 * rb + 16, 128 * lb : 128 * lb + 128] = acc_a[4 * rb + lb]
    scaled = sum_a[...] * gain_v[...]
    dots = jnp.mean(scaled * values, axis=1, keepdims=True)
    kv_row[:, :LATENT] = (inverse * (scaled - values * inverse * inverse * dots)).astype(BF16)
    rope = acc_a[8]
    other = jnp.where(front, pltpu.roll(rope, 96, 1), pltpu.roll(rope, 32, 1))
    rotated = rope * cosine + other * sine
    kv_row[0:16, LATENT:KVW] = rotated[:, :ROPE].astype(BF16)
    kv_row[16:32, LATENT:KVW] = pltpu.roll(rotated, 64, 1)[:, :ROPE].astype(BF16)
    kva[own_rows, :] = dot(kv_row[...], pick_v[...], NN).astype(BF16)

    def rows_of(head):
        return pl.ds(pl.multiple_of(head * ROWS, ROWS), ROWS)

    def gather_copy(head, send, recv, peer):
        rows = kva.at[rows_of(head), :]
        copy = pltpu.make_async_remote_copy(rows, rows, send, recv, device_id=peer, device_id_type=MESH)
        copy.start()
        return copy

    g_copies = {}
    for d in far_first(nx):
        g_copies[d] = gather_copy(h, gs_sem.at[d], gr_sem.at[d], x_peer[d])
    f_copies = {0: gather_copy(h, fs_sem.at[0], fr_sem.at[0], z_peer)}
    for d in reversed(far_first(nx)):
        g_copies[d].wait_recv()
        f_copies[d] = gather_copy(zl * nx + (x - d + nx) % nx, fs_sem.at[d], fr_sem.at[d], z_peer)
    for d in f_copies:
        f_copies[d].wait_recv()

    product = dot(kva[...], hidden_v[...], TT)
    for k in range(2):
        for j in range(ny):
            at = (k * ny + j) * block
            w_f32[k, j] = product[at : at + block].reshape(w_f32.shape[2:])
    csend[...] = w_f32[1 - core].astype(BF16)
    c_copies, y_copies = {}, {}
    order = far_first(ny) + [0]
    for d in order:
        to = (y + d) % ny
        c_copies[d] = pltpu.make_async_remote_copy(
            csend.at[to], crecv.at[to], cs_sem.at[d], cr_sem.at[d], device_id=core_peer, device_id_type=MESH
        )
        c_copies[d].start()
    total = None
    for d in order:
        to = (y + d) % ny
        c_copies[d].wait_recv()
        total = w_f32[core, to] + crecv[to].astype(F32)
        if d != 0:
            ysend[d] = total.astype(BF16)
            y_copies[d] = pltpu.make_async_remote_copy(
                ysend.at[d], yrecv.at[d], ys_sem.at[d], yr_sem.at[d], device_id=y_peer[d], device_id_type=MESH
            )
            y_copies[d].start()

    hid_v[...] = dot(down_p[...], kva[...], NT).astype(BF16)
    out_copy = pltpu.make_async_copy(hid_v, hidden_out, out_sem)
    out_copy.start()

    for d in far_first(ny):
        y_copies[d].wait_recv()
        total = total + yrecv[d].astype(F32)
    acc_c[...] = total.reshape(acc_c.shape)
    for k in range(nzh):
        piece = acc_c[k * own : k * own + own, :]
        hi_f32[k, 0:own, :] = piece
        hi_send[k, 0:own, :] = piece.astype(BF16)
    h_copies = {}
    for d in far_first(nzh):
        to = (zh + d) % nzh
        h_copies[d] = pltpu.make_async_remote_copy(
            hi_send.at[to], hi_recv.at[d], hs_sem.at[d], hr_sem.at[d], device_id=h_peer[d], device_id_type=MESH
        )
        h_copies[d].start()
    result = hi_f32[zh, 0:own, :]
    for d in far_first(nzh):
        h_copies[d].wait_recv()
        result = result + hi_recv[d, 0:own, :].astype(F32)
    weight_out[...] = result

    for copies in (z_copies, x_copies, g_copies, f_copies, c_copies, y_copies, h_copies):
        for copy in copies.values():
            copy.wait_send()
    out_copy.wait()


def on_device(lay, *args):
    key, value, rope, key_lift, value_lift, latent, gain, docs, hidden, down = args
    half = lay.seq // 2
    nx, ny, nzh = lay.nx, lay.ny, lay.nzh
    hidden = hidden.T
    cols = hidden.shape[0]
    rows8 = (lay.block // 8, 8, cols)
    dma = pltpu.SemaphoreType.DMA
    any_spec = pl.BlockSpec(memory_space=pl.ANY)
    scratch = [
        pltpu.VMEM((2, half, key.shape[1]), BF16),
        pltpu.VMEM((2, half, value.shape[1]), BF16),
        pltpu.VMEM((2, half, rope.shape[1]), BF16),
        pltpu.VMEM(key_lift.shape, BF16),
        pltpu.VMEM(value_lift.shape, BF16),
        pltpu.VMEM((ROWS, LATENT), BF16),
        pltpu.VMEM((1, LATENT), F32),
        pltpu.SMEM(docs.shape, jnp.int32),
        pltpu.VMEM(hidden.shape, BF16),
        pltpu.VMEM(down.shape, BF16),
        dma((13,)),
        pltpu.VMEM((rope.shape[1], 128), BF16),
        pltpu.VMEM((KVW, lay.kp), BF16),
        pltpu.VMEM((down.shape[0], lay.kp), BF16),
        pltpu.VMEM((nx, TILES, 16, 128), F32),
        pltpu.VMEM((nx, TILES, 16, 128), BF16),
        pltpu.VMEM((nx, TILES, 16, 128), BF16),
        pltpu.VMEM((nx, TILES, 16, 128), BF16),
        pltpu.VMEM((nx, TILES, 16, 128), BF16),
        pltpu.VMEM((TILES, 16, 128), F32),
        pltpu.VMEM((ROWS, LATENT), F32),
        pltpu.VMEM((ROWS, KVW), BF16),
        pltpu.VMEM((lay.seq, lay.kp), BF16),
        pltpu.VMEM((2, ny, *rows8), F32),
        pltpu.VMEM((ny, *rows8), BF16),
        pltpu.VMEM((ny, *rows8), BF16),
        pltpu.VMEM((ny, *rows8), BF16),
        pltpu.VMEM((ny, *rows8), BF16),
        pltpu.VMEM((lay.block, cols), F32),
        pltpu.VMEM((nzh, lay.ownp, cols), F32),
        pltpu.VMEM((nzh, lay.ownp, cols), BF16),
        pltpu.VMEM((nzh, lay.ownp, cols), BF16),
        pltpu.VMEM((cols, lay.seq), BF16),
        dma,
        *[dma((nx,))] * 8,
        *[dma((ny,))] * 4,
        *[dma((nzh,))] * 2,
    ]
    hidden_grad, weight_grad = pl.pallas_call(
        functools.partial(kernel, lay),
        out_shape=(
            jax.ShapeDtypeStruct((cols, lay.seq), BF16),
            jax.ShapeDtypeStruct((lay.own, cols), F32),
        ),
        in_specs=[any_spec] * 10,
        out_specs=(any_spec, pl.BlockSpec(memory_space=pltpu.VMEM)),
        scratch_shapes=scratch,
        compiler_params=pltpu.CompilerParams(
            collective_id=0, has_side_effects=True, vmem_limit_bytes=60 * 1024 * 1024
        ),
        name="latent_backward",
    )(key, value, rope, key_lift, value_lift, latent, gain.reshape(1, -1), docs, hidden, down)
    return hidden_grad.T, weight_grad


def solution(mesh, lay=Layout(4, 8, 8)):
    return jax.shard_map(
        functools.partial(on_device, lay),
        mesh=mesh,
        in_specs=(
            P("group", "head"),
            P("group", "head"),
            P("group", "head"),
            P(None, "head"),
            P(None, "head"),
            P("group", None),
            P(),
            P("group", None),
            P("group", "head"),
            P("head", None),
        ),
        out_specs=(P("group", "head"), P("group", "head")),
        check_vma=False,
    )
```

```python
import functools

import jax
import jax.numpy as jnp
from jax import lax
from jax.experimental import pallas as pl
from jax.experimental.pallas import tpu as pltpu
from jax.sharding import PartitionSpec as P

LATENT = 512
ROPE = 64
KVW = LATENT + ROPE
ROWS = 32
TILES = KVW * ROWS // (16 * 128)
MESH = pl.DeviceIdType.MESH
NT = (((1,), (1,)), ((), ()))
TT = (((0,), (1,)), ((), ()))
NN = (((1,), (0,)), ((), ()))
F32 = jnp.float32
BF16 = jnp.bfloat16


class Layout:
    def __init__(self, nzh, ny, nx):
        self.nzh, self.ny, self.nx = nzh, ny, nx
        self.heads = 2 * nx
        self.groups = 2 * ny * nzh
        self.seq = ROWS * self.heads
        self.own = KVW // self.groups
        self.block = -(-nzh * self.own // 8) * 8
        self.used = 2 * ny * self.block
        self.kp = -(-self.used // 128) * 128
        self.ownp = -(-self.own // 16) * 16


def far_first(n):
    return sorted(range(1, n), key=lambda d: (-min(d, n - d), d))


def remote(src, dst, send, recv, peer):
    return pltpu.make_async_remote_copy(src, dst, send, recv, device_id=peer, device_id_type=MESH)


class Ring:
    PLAN = {"far": (0, 3, 1), "raf": (1, -3, -1), "add": (3, 2, 2), "dda": (4, -2, -2), "one": (5, 1, 1), "eno": (6, -1, -1)}

    def __init__(self, peer, send, recv, send_sem, recv_sem, split):
        self.peer, self.send, self.recv, self.split = peer, send, recv, split
        self.send_sem, self.recv_sem = send_sem, recv_sem
        self.copies = {}

    def start(self, name, src, dst, sem, hop):
        self.copies[name] = remote(src, dst, self.send_sem, self.recv_sem.at[sem], self.peer[hop])
        self.copies[name].start()

    def put(self, name, term):
        slot, _, hop = self.PLAN[name]
        self.send[slot] = term.astype(BF16)
        self.start(name, self.send.at[slot], self.recv.at[slot], slot, hop)

    def put_opposite(self, term):
        self.send[2] = term.astype(BF16)
        first, second = pl.ds(0, self.split), pl.ds(self.split, self.send.shape[1] - self.split)
        self.start("first", self.send.at[2, first], self.recv.at[2, first], 2, 2)
        self.start("second", self.send.at[2, second], self.recv.at[2, second], 7, -2)

    def take(self, name):
        self.copies[name].wait_recv()
        return self.recv[self.PLAN[name][0]].astype(F32)

    def relay(self, name, term_ref, index):
        far, part = ("far", "first") if name == "add" else ("raf", "second")
        self.copies[far].wait_recv()
        self.copies[part].wait_recv()
        rows = pl.ds(0, self.split) if name == "add" else pl.ds(self.split, self.send.shape[1] - self.split)
        slot = self.PLAN[far][0]
        term_ref[index] = term_ref[index] + self.recv[slot].astype(F32)
        whole = term_ref.at[index]
        whole[rows] = whole[rows] + self.recv[2, rows].astype(F32)
        self.put(name, term_ref[index])

    def reduce(self, size, me, ready, term_ref):
        def at(offset):
            return (me + offset + size) % size

        def term(offset):
            ready(offset % size, at(offset))
            return term_ref[at(offset)]

        if size == 1:
            return term(0)
        self.put_opposite(term(4))
        self.put("far", term(3))
        self.put("raf", term(-3))
        ready(2, at(2))
        ready(6, at(-2))
        self.relay("add", term_ref, at(2))
        self.relay("dda", term_ref, at(-2))
        self.put("one", term(1))
        self.put("eno", term(-1))
        return term(0)

    def collect(self, size, total):
        if size == 1:
            return total
        for name in ("one", "eno", "add", "dda"):
            total = total + self.take(name)
        return total

    def finish(self, size):
        if size > 1:
            remote(self.send, self.recv, self.send_sem, self.recv_sem.at[0], self.peer[1]).wait_send()


def dot(a, b, dims):
    return lax.dot_general(a, b, dims, preferred_element_type=F32)


def kernel(
    lay,
    key_hbm,
    value_hbm,
    rope_hbm,
    key_lift_hbm,
    value_lift_hbm,
    latent_hbm,
    gain_hbm,
    docs_hbm,
    hidden_hbm,
    down_hbm,
    hidden_out,
    weight_out,
    key_v,
    value_v,
    rope_v,
    key_lift_v,
    value_lift_v,
    latent_v,
    gain_v,
    docs_s,
    hidden_v,
    down_v,
    load_sem,
    fold_v,
    pick_v,
    down_p,
    own_a,
    zsend,
    zrecv,
    xsend,
    xrecv,
    acc_a,
    sum_a,
    kv_row,
    kva,
    w_f32,
    csend,
    crecv,
    ysend,
    yrecv,
    acc_c,
    hi_f32,
    hi_send,
    hi_recv,
    zs_sem,
    zr_sem,
    xs_sem,
    xr_sem,
    gs_sem,
    gr_sem,
    fs_sem,
    fr_sem,
    cs_sem,
    cr_sem,
    ys_sem,
    yr_sem,
    hs_sem,
    hr_sem,
):
    nx, ny, nzh = lay.nx, lay.ny, lay.nzh
    half = lay.seq // 2
    g = lax.axis_index("group")
    h = lax.axis_index("head")
    core, y, zh = g % 2, (g // 2) % ny, g // (2 * ny)
    x, zl = h % nx, h // nx

    z_peer = (g, (1 - zl) * nx + x)
    core_peer = (g + 1 - 2 * core, h)
    near = (2, -2, 1, -1)
    x_peer = {d: (g, zl * nx + (x + d + nx) % nx) for d in near if nx > 1}
    y_peer = {d: ((zh * ny + (y + d + ny) % ny) * 2 + core, h) for d in near if ny > 1}
    h_peer = {d: ((((zh + d) % nzh) * ny + y) * 2 + core, h) for d in range(1, nzh)}
    peers = [z_peer, core_peer, *x_peer.values(), *y_peer.values(), *h_peer.values()]

    theirs = pl.ds(pl.multiple_of((1 - zl) * half, half), half)
    mine = pl.ds(pl.multiple_of(zl * half, half), half)
    own_rows = pl.ds(pl.multiple_of(h * ROWS, ROWS), ROWS)
    loads = []

    def load(src, dst):
        copy = pltpu.make_async_copy(src, dst, load_sem.at[len(loads)])
        copy.start()
        loads.append(copy)
        return copy

    first = [
        load(key_lift_hbm, key_lift_v),
        load(key_hbm.at[theirs, :], key_v.at[0]),
        load(value_lift_hbm, value_lift_v),
        load(value_hbm.at[theirs, :], value_v.at[0]),
        load(rope_hbm.at[theirs, :], rope_v.at[0]),
    ]
    second = [
        load(key_hbm.at[mine, :], key_v.at[1]),
        load(value_hbm.at[mine, :], value_v.at[1]),
        load(rope_hbm.at[mine, :], rope_v.at[1]),
    ]
    third = [
        load(down_hbm, down_v),
        load(latent_hbm.at[own_rows, :], latent_v),
        load(gain_hbm, gain_v),
        load(docs_hbm, docs_s),
        load(hidden_hbm, hidden_v),
    ]

    barrier = pltpu.get_barrier_semaphore()
    for peer in peers:
        pl.semaphore_signal(barrier, inc=1, device_id=peer, device_id_type=MESH)

    width = rope_v.shape[2]
    fold_row = lax.broadcasted_iota(jnp.int32, (width, 128), 0)
    fold_col = lax.broadcasted_iota(jnp.int32, (width, 128), 1)
    fold_v[...] = jnp.where((fold_row & 63) == (fold_col & 63), 1.0, 0.0).astype(BF16)
    low = lax.broadcasted_iota(jnp.int32, (16, 128), 1) < 64

    def partial(part):
        terms = dot(key_v[part], key_lift_v[...], NT) + dot(value_v[part], value_lift_v[...], NT)
        return terms, dot(rope_v[part], fold_v[...], NN)

    def tiles(terms, ropes, chunk):
        base = chunk * ROWS
        for block in range(2):
            rows = slice(base + 16 * block, base + 16 * block + 16)
            for lane in range(4):
                yield 4 * block + lane, terms[rows, 128 * lane : 128 * lane + 128]
        yield 8, jnp.where(low, ropes[base : base + 16], ropes[base + 16 : base + 32])

    for copy in first:
        copy.wait()
    terms, ropes = partial(0)
    for chunk in range(nx):
        for i, tile in tiles(terms, ropes, chunk):
            zsend[chunk, i] = tile.astype(BF16)
    pl.semaphore_wait(barrier, len(peers))

    order = [0] if nx == 1 else [4, 3, 5, 2, 6, 1, 7, 0]
    z_copies = {}
    for d in order:
        to = (x + d) % nx
        z_copies[d] = remote(zsend.at[to], zrecv.at[to], zs_sem, zr_sem.at[d], z_peer)
        z_copies[d].start()
    for copy in second:
        copy.wait()
    terms, ropes = partial(1)
    for chunk in range(nx):
        for i, tile in tiles(terms, ropes, chunk):
            own_a[chunk, i] = tile

    for copy in third:
        copy.wait()
    block, own = lay.block, lay.own
    col = lax.broadcasted_iota(jnp.int32, (KVW, lay.kp), 1)
    row = lax.broadcasted_iota(jnp.int32, (KVW, lay.kp), 0)
    chunk_of = jnp.zeros_like(col)
    for k in range(1, 2 * ny):
        chunk_of = chunk_of + jnp.where(col >= k * block, 1, 0)
    q = col - chunk_of * block
    hi_of = jnp.zeros_like(col)
    for k in range(1, nzh):
        hi_of = hi_of + jnp.where(q >= k * own, 1, 0)
    core_of = jnp.where(chunk_of >= ny, 1, 0)
    source = ((hi_of * ny + chunk_of - core_of * ny) * 2 + core_of) * own + q - hi_of * own
    picked = (row == source) & (q < nzh * own) & (col < lay.used)
    pick_v[...] = jnp.where(picked, 1.0, 0.0).astype(BF16)
    down_p[...] = dot(down_v[...], pick_v[...], NN).astype(BF16)

    lane = lax.broadcasted_iota(jnp.int32, (16, 128), 1)
    token = h * ROWS + lax.broadcasted_iota(jnp.int32, (16, 128), 0) + jnp.where(low, 0, 16)
    start = jnp.zeros_like(token)
    end = jnp.int32(0)
    for k in range(docs_s.shape[1]):
        end = end + docs_s[0, k]
        start = jnp.maximum(start, jnp.where(token >= end, end, 0))
    position = (token - start).astype(F32)
    pair = (lane & 31).astype(F32)
    angle = position * jnp.exp(pair * (-2.0 / ROPE * 9.210340371976184))
    cosine, sine = jnp.cos(angle), jnp.sin(angle)
    front = (lane & 32) == 0
    sine = jnp.where(front, sine, -sine)
    values = latent_v[...].astype(F32)
    inverse = lax.rsqrt(jnp.mean(values * values, axis=1, keepdims=True) + 1e-06)

    def from_z(offset, owner):
        z_copies[offset].wait_recv()
        own_a[owner] = own_a[owner] + zrecv[owner].astype(F32)

    x_ring = Ring(x_peer, xsend, xrecv, xs_sem, xr_sem, 5)
    mine_a = x_ring.reduce(nx, x, from_z, own_a)
    acc_a[...] = x_ring.collect(nx, mine_a)

    for rb in range(2):
        for lb in range(4):
            sum_a[16 * rb : 16 * rb + 16, 128 * lb : 128 * lb + 128] = acc_a[4 * rb + lb]
    scaled = sum_a[...] * gain_v[...]
    dots = jnp.mean(scaled * values, axis=1, keepdims=True)
    kv_row[:, :LATENT] = (inverse * (scaled - values * inverse * inverse * dots)).astype(BF16)
    rope = acc_a[8]
    other = jnp.where(front, pltpu.roll(rope, 96, 1), pltpu.roll(rope, 32, 1))
    rotated = rope * cosine + other * sine
    kv_row[0:16, LATENT:KVW] = rotated[:, :ROPE].astype(BF16)
    kv_row[16:32, LATENT:KVW] = pltpu.roll(rotated, 64, 1)[:, :ROPE].astype(BF16)
    kva[own_rows, :] = dot(kv_row[...], pick_v[...], NN).astype(BF16)

    def block_at(offset, part=None):
        head = zl * nx + (x + offset + nx) % nx
        first, size = (0, ROWS) if part is None else (part * ROWS // 2, ROWS // 2)
        return kva.at[pl.ds(pl.multiple_of(head * ROWS + first, size), size), :]

    g_copies, f_copies = {}, {}

    def along(name, rows, sem, hop):
        g_copies[name] = remote(rows, rows, gs_sem, gr_sem.at[sem], x_peer[hop])
        g_copies[name].start()

    def across(rows):
        sem = len(f_copies)
        f_copies[sem] = remote(rows, rows, fs_sem, fr_sem.at[sem], z_peer)
        f_copies[sem].start()

    if nx > 1:
        for sem, hop in enumerate(near):
            along(hop, block_at(0), sem, hop)
    across(block_at(0))
    if nx > 1:
        g_copies[2].wait_recv()
        along("far", block_at(-2), 4, 1)
        along("first", block_at(-2, 0), 5, 2)
        g_copies[-2].wait_recv()
        along("raf", block_at(2), 6, -1)
        along("second", block_at(2, 1), 7, -2)
        for hop in (1, -1):
            g_copies[hop].wait_recv()
            across(block_at(-hop))
        across(block_at(-2))
        across(block_at(2))
        g_copies["far"].wait_recv()
        across(block_at(-3))
        g_copies["raf"].wait_recv()
        across(block_at(3))
        g_copies["first"].wait_recv()
        across(block_at(4, 0))
        g_copies["second"].wait_recv()
        across(block_at(4, 1))
    for copy in f_copies.values():
        copy.wait_recv()

    product = dot(kva[...], hidden_v[...], TT)
    for k in range(2):
        for j in range(ny):
            at = (k * ny + j) * block
            w_f32[k, j] = product[at : at + block].reshape(w_f32.shape[2:])
    csend[...] = w_f32[1 - core].astype(BF16)
    c_copies = {}
    order = [0] if ny == 1 else [4, 3, 5, 2, 6, 1, 7, 0]
    for d in order:
        to = (y + d) % ny
        c_copies[d] = remote(csend.at[to], crecv.at[to], cs_sem, cr_sem.at[d], core_peer)
        c_copies[d].start()

    own_c = w_f32.at[core]

    def from_core(offset, owner):
        c_copies[offset].wait_recv()
        own_c[owner] = own_c[owner] + crecv[owner].astype(F32)

    y_ring = Ring(y_peer, ysend, yrecv, ys_sem, yr_sem, (block // 8 + 1) // 2)
    mine_c = y_ring.reduce(ny, y, from_core, own_c)
    hidden_out[...] = dot(down_p[...], kva[...], NT).astype(BF16)
    total = y_ring.collect(ny, mine_c)
    acc_c[...] = total.reshape(acc_c.shape)
    for k in range(nzh):
        piece = acc_c[k * own : k * own + own, :]
        hi_f32[k, 0:own, :] = piece
        hi_send[k, 0:own, :] = piece.astype(BF16)
    h_copies = {}
    for d in far_first(nzh):
        to = (zh + d) % nzh
        h_copies[d] = remote(hi_send.at[to], hi_recv.at[d], hs_sem, hr_sem.at[d], h_peer[d])
        h_copies[d].start()
    result = hi_f32[zh, 0:own, :]
    for d in far_first(nzh):
        h_copies[d].wait_recv()
        result = result + hi_recv[d, 0:own, :].astype(F32)
    weight_out[...] = result

    remote(zsend, zrecv, zs_sem, zr_sem.at[0], z_peer).wait_send()
    x_ring.finish(nx)
    if nx > 1:
        sent = kva.at[pl.ds(0, 7 * ROWS), :]
        remote(sent, sent, gs_sem, gr_sem.at[0], x_peer[1]).wait_send()
    passed = kva.at[pl.ds(0, nx * ROWS), :]
    remote(passed, passed, fs_sem, fr_sem.at[0], z_peer).wait_send()
    remote(csend, crecv, cs_sem, cr_sem.at[0], core_peer).wait_send()
    y_ring.finish(ny)
    if nzh > 1:
        sent = pl.ds(1, nzh - 1)
        remote(hi_send.at[sent], hi_recv.at[sent], hs_sem, hr_sem.at[1], core_peer).wait_send()


def on_device(lay, *args):
    key, value, rope, key_lift, value_lift, latent, gain, docs, hidden, down = args
    half = lay.seq // 2
    nx, ny, nzh = lay.nx, lay.ny, lay.nzh
    hidden = hidden.T
    cols = hidden.shape[0]
    rows8 = (lay.block // 8, 8, cols)
    dma = pltpu.SemaphoreType.DMA
    any_spec = pl.BlockSpec(memory_space=pl.ANY)
    scratch = [
        pltpu.VMEM((2, half, key.shape[1]), BF16),
        pltpu.VMEM((2, half, value.shape[1]), BF16),
        pltpu.VMEM((2, half, rope.shape[1]), BF16),
        pltpu.VMEM(key_lift.shape, BF16),
        pltpu.VMEM(value_lift.shape, BF16),
        pltpu.VMEM((ROWS, LATENT), BF16),
        pltpu.VMEM((1, LATENT), F32),
        pltpu.SMEM(docs.shape, jnp.int32),
        pltpu.VMEM(hidden.shape, BF16),
        pltpu.VMEM(down.shape, BF16),
        dma((13,)),
        pltpu.VMEM((rope.shape[1], 128), BF16),
        pltpu.VMEM((KVW, lay.kp), BF16),
        pltpu.VMEM((down.shape[0], lay.kp), BF16),
        pltpu.VMEM((nx, TILES, 16, 128), F32),
        pltpu.VMEM((nx, TILES, 16, 128), BF16),
        pltpu.VMEM((nx, TILES, 16, 128), BF16),
        pltpu.VMEM((7, TILES, 16, 128), BF16),
        pltpu.VMEM((7, TILES, 16, 128), BF16),
        pltpu.VMEM((TILES, 16, 128), F32),
        pltpu.VMEM((ROWS, LATENT), F32),
        pltpu.VMEM((ROWS, KVW), BF16),
        pltpu.VMEM((lay.seq, lay.kp), BF16),
        pltpu.VMEM((2, ny, *rows8), F32),
        pltpu.VMEM((ny, *rows8), BF16),
        pltpu.VMEM((ny, *rows8), BF16),
        pltpu.VMEM((7, *rows8), BF16),
        pltpu.VMEM((7, *rows8), BF16),
        pltpu.VMEM((lay.block, cols), F32),
        pltpu.VMEM((nzh, lay.ownp, cols), F32),
        pltpu.VMEM((nzh, lay.ownp, cols), BF16),
        pltpu.VMEM((nzh, lay.ownp, cols), BF16),
        dma,
        dma((8,)),
        dma,
        dma((8,)),
        dma,
        dma((8,)),
        dma,
        dma((9,)),
        dma,
        dma((8,)),
        dma,
        dma((8,)),
        dma,
        dma((nzh,)),
    ]
    hidden_grad, weight_grad = pl.pallas_call(
        functools.partial(kernel, lay),
        out_shape=(
            pltpu.VMEM((cols, lay.seq), BF16),
            pltpu.VMEM((lay.own, cols), F32),
        ),
        in_specs=[any_spec] * 10,
        out_specs=(pl.BlockSpec(memory_space=pltpu.VMEM),) * 2,
        scratch_shapes=scratch,
        compiler_params=pltpu.CompilerParams(
            collective_id=0, has_side_effects=True, vmem_limit_bytes=60 * 1024 * 1024
        ),
        name="latent_backward",
    )(key, value, rope, key_lift, value_lift, latent, gain.reshape(1, -1), docs, hidden, down)
    return hidden_grad.T, weight_grad


def solution(mesh, lay=Layout(4, 8, 8)):
    return jax.shard_map(
        functools.partial(on_device, lay),
        mesh=mesh,
        in_specs=(
            P("group", "head"),
            P("group", "head"),
            P("group", "head"),
            P(None, "head"),
            P(None, "head"),
            P("group", None),
            P(),
            P("group", None),
            P("group", "head"),
            P("head", None),
        ),
        out_specs=(P("group", "head"), P("group", "head")),
        check_vma=False,
    )
```

```python
import functools

import jax
import jax.numpy as jnp
from jax import lax
from jax.experimental import pallas as pl
from jax.experimental.pallas import tpu as pltpu
from jax.sharding import PartitionSpec as P

LATENT = 512
ROPE = 64
KVW = LATENT + ROPE
ROWS = 32
TILES = KVW * ROWS // (16 * 128)
MESH = pl.DeviceIdType.MESH
NT = (((1,), (1,)), ((), ()))
TT = (((0,), (1,)), ((), ()))
NN = (((1,), (0,)), ((), ()))
F32 = jnp.float32
BF16 = jnp.bfloat16


class Layout:
    def __init__(self, nzh, ny, nx):
        self.nzh, self.ny, self.nx = nzh, ny, nx
        self.heads = 2 * nx
        self.groups = 2 * ny * nzh
        self.seq = ROWS * self.heads
        self.own = KVW // self.groups
        self.block = -(-nzh * self.own // 8) * 8
        self.used = 2 * ny * self.block
        self.kp = -(-self.used // 128) * 128
        self.ownp = -(-self.own // 16) * 16


def far_first(n):
    return sorted(range(1, n), key=lambda d: (-min(d, n - d), d))


def remote(src, dst, send, recv, peer):
    return pltpu.make_async_remote_copy(src, dst, send, recv, device_id=peer, device_id_type=MESH)


class Ring:
    PLAN = {"far": (0, 3, 1), "raf": (1, -3, -1), "add": (3, 2, 2), "dda": (4, -2, -2), "one": (5, 1, 1), "eno": (6, -1, -1)}

    def __init__(self, peer, send, recv, send_sem, recv_sem, split, direct=False):
        self.peer, self.send, self.recv, self.split = peer, send, recv, split
        self.direct = direct
        self.send_sem, self.recv_sem = send_sem, recv_sem
        self.copies = {}

    def start(self, name, src, dst, sem, hop):
        self.copies[name] = remote(src, dst, self.send_sem, self.recv_sem.at[sem], self.peer[hop])
        self.copies[name].start()

    def put(self, name, term):
        slot, offset, hop = self.PLAN[name]
        hop = offset if self.direct else hop
        self.send[slot] = term.astype(BF16)
        self.start(name, self.send.at[slot], self.recv.at[slot], slot, hop)

    def put_opposite(self, term):
        self.send[2] = term.astype(BF16)
        first, second = pl.ds(0, self.split), pl.ds(self.split, self.send.shape[1] - self.split)
        self.start("first", self.send.at[2, first], self.recv.at[2, first], 2, 2)
        self.start("second", self.send.at[2, second], self.recv.at[2, second], 7, -2)

    def take(self, name):
        self.copies[name].wait_recv()
        return self.recv[self.PLAN[name][0]].astype(F32)

    def relay(self, name, term_ref, index):
        far, part = ("far", "first") if name == "add" else ("raf", "second")
        if not self.direct:
            self.copies[far].wait_recv()
        self.copies[part].wait_recv()
        rows = pl.ds(0, self.split) if name == "add" else pl.ds(self.split, self.send.shape[1] - self.split)
        if not self.direct:
            term_ref[index] = term_ref[index] + self.recv[self.PLAN[far][0]].astype(F32)
        whole = term_ref.at[index]
        whole[rows] = whole[rows] + self.recv[2, rows].astype(F32)
        self.put(name, term_ref[index])

    def reduce(self, size, me, ready, term_ref, near_first):
        def at(offset):
            return (me + offset + size) % size

        def term(offset):
            ready(offset % size, at(offset))
            return term_ref[at(offset)]

        if size == 1:
            return term(0)
        if near_first:
            self.put("one", term(1))
            self.put("eno", term(-1))
        self.put_opposite(term(4))
        self.put("far", term(3))
        self.put("raf", term(-3))
        if not near_first:
            self.put("one", term(1))
            self.put("eno", term(-1))
        ready(2, at(2))
        ready(6, at(-2))
        self.relay("add", term_ref, at(2))
        self.relay("dda", term_ref, at(-2))
        return term(0)

    def collect(self, size, total):
        if size == 1:
            return total
        for name in ("one", "eno", *(("far", "raf") if self.direct else ()), "add", "dda"):
            total = total + self.take(name)
        return total

    def finish(self, size):
        if size > 1:
            remote(self.send, self.recv, self.send_sem, self.recv_sem.at[0], self.peer[1]).wait_send()


def dot(a, b, dims):
    return lax.dot_general(a, b, dims, preferred_element_type=F32)


def kernel(
    lay,
    key_hbm,
    value_hbm,
    rope_hbm,
    key_lift_hbm,
    value_lift_hbm,
    latent_hbm,
    gain_hbm,
    docs_hbm,
    hidden_hbm,
    down_hbm,
    hidden_out,
    weight_out,
    key_v,
    value_v,
    rope_v,
    key_lift_v,
    value_lift_v,
    latent_v,
    gain_v,
    docs_s,
    hidden_v,
    down_v,
    load_sem,
    fold_v,
    pick_v,
    down_p,
    own_a,
    zsend,
    zrecv,
    precv,
    zsum,
    xsend,
    xrecv,
    acc_a,
    sum_a,
    kv_row,
    kva,
    w_f32,
    csend,
    crecv,
    ysend,
    yrecv,
    acc_c,
    hi_f32,
    hi_send,
    hi_recv,
    zs_sem,
    zr_sem,
    ps_sem,
    pr_sem,
    xs_sem,
    xr_sem,
    gs_sem,
    gr_sem,
    fs_sem,
    fr_sem,
    cs_sem,
    cr_sem,
    ys_sem,
    yr_sem,
    hs_sem,
    hr_sem,
):
    nx, ny, nzh = lay.nx, lay.ny, lay.nzh
    half = lay.seq // 2
    g = lax.axis_index("group")
    h = lax.axis_index("head")
    core, y, zh = g % 2, (g // 2) % ny, g // (2 * ny)
    x, zl = h % nx, h // nx

    z_peer = (g, (1 - zl) * nx + x)
    core_peer = (g + 1 - 2 * core, h)
    near = (2, -2, 1, -1)
    x_peer = {d: (g, zl * nx + (x + d + nx) % nx) for d in (3, -3, *near) if nx > 1}
    y_peer = {d: ((zh * ny + (y + d + ny) % ny) * 2 + core, h) for d in near if ny > 1}
    h_peer = {d: ((((zh + d) % nzh) * ny + y) * 2 + core, h) for d in range(1, nzh)}
    peers = [z_peer, core_peer, *x_peer.values(), *y_peer.values(), *h_peer.values()]

    theirs = pl.ds(pl.multiple_of((1 - zl) * half, half), half)
    mine = pl.ds(pl.multiple_of(zl * half, half), half)
    own_rows = pl.ds(pl.multiple_of(h * ROWS, ROWS), ROWS)
    loads = []

    def load(src, dst):
        copy = pltpu.make_async_copy(src, dst, load_sem.at[len(loads)])
        copy.start()
        loads.append(copy)
        return copy

    first = [load(key_lift_hbm, key_lift_v), load(key_hbm.at[theirs, :], key_v.at[0])]
    second = [
        load(value_lift_hbm, value_lift_v),
        load(value_hbm.at[theirs, :], value_v.at[0]),
        load(rope_hbm.at[theirs, :], rope_v.at[0]),
    ]

    barrier = pltpu.get_barrier_semaphore()
    for peer in peers:
        pl.semaphore_signal(barrier, inc=1, device_id=peer, device_id_type=MESH)

    width = rope_v.shape[2]
    fold_row = lax.broadcasted_iota(jnp.int32, (width, 128), 0)
    fold_col = lax.broadcasted_iota(jnp.int32, (width, 128), 1)
    fold_v[...] = jnp.where((fold_row & 63) == (fold_col & 63), 1.0, 0.0).astype(BF16)
    low = lax.broadcasted_iota(jnp.int32, (16, 128), 1) < 64

    def tiles(terms, ropes, chunk):
        base = chunk * ROWS
        for block in range(2):
            rows = slice(base + 16 * block, base + 16 * block + 16)
            for lane in range(4):
                yield 4 * block + lane, terms[rows, 128 * lane : 128 * lane + 128]
        yield 8, jnp.where(low, ropes[base : base + 16], ropes[base + 16 : base + 32])

    for copy in first:
        copy.wait()
    terms = dot(key_v[0], key_lift_v[...], NT)
    for copy in second:
        copy.wait()
    third = [
        load(key_hbm.at[mine, :], key_v.at[1]),
        load(value_hbm.at[mine, :], value_v.at[1]),
        load(rope_hbm.at[mine, :], rope_v.at[1]),
    ]
    fourth = [
        load(down_hbm, down_v),
        load(latent_hbm.at[own_rows, :], latent_v),
        load(gain_hbm, gain_v),
        load(docs_hbm, docs_s),
        load(hidden_hbm, hidden_v),
    ]
    terms = terms + dot(value_v[0], value_lift_v[...], NT)
    ropes = dot(rope_v[0], fold_v[...], NN)
    for chunk in range(nx):
        for i, tile in tiles(terms, ropes, chunk):
            zsend[chunk, i] = tile.astype(BF16)
    pl.semaphore_wait(barrier, len(peers))

    order = [0] if nx == 1 else [4, 3, 5, 2, 6]
    z_copies, p_copies = {}, {}
    for d in order:
        to = (x + d) % nx
        z_copies[d] = remote(zsend.at[to], zrecv.at[to], zs_sem, zr_sem.at[d], z_peer)
        z_copies[d].start()
        if d == 4:
            for slot, hop in enumerate((1, -1)):
                to = (x + hop + nx) % nx
                p_copies[slot] = remote(zsend.at[to], precv.at[slot], ps_sem, pr_sem.at[slot], x_peer[hop])
                p_copies[slot].start()
    for copy in third:
        copy.wait()
    terms = dot(key_v[1], key_lift_v[...], NT) + dot(value_v[1], value_lift_v[...], NT)
    ropes = dot(rope_v[1], fold_v[...], NN)
    for chunk in range(nx):
        for i, tile in tiles(terms, ropes, chunk):
            own_a[chunk, i] = tile

    for copy in fourth:
        copy.wait()
    block, own = lay.block, lay.own
    col = lax.broadcasted_iota(jnp.int32, (KVW, lay.kp), 1)
    row = lax.broadcasted_iota(jnp.int32, (KVW, lay.kp), 0)
    chunk_of = jnp.zeros_like(col)
    for k in range(1, 2 * ny):
        chunk_of = chunk_of + jnp.where(col >= k * block, 1, 0)
    q = col - chunk_of * block
    hi_of = jnp.zeros_like(col)
    for k in range(1, nzh):
        hi_of = hi_of + jnp.where(q >= k * own, 1, 0)
    core_of = jnp.where(chunk_of >= ny, 1, 0)
    source = ((hi_of * ny + chunk_of - core_of * ny) * 2 + core_of) * own + q - hi_of * own
    picked = (row == source) & (q < nzh * own) & (col < lay.used)
    pick_v[...] = jnp.where(picked, 1.0, 0.0).astype(BF16)
    down_p[...] = dot(down_v[...], pick_v[...], NN).astype(BF16)

    lane = lax.broadcasted_iota(jnp.int32, (16, 128), 1)
    token = h * ROWS + lax.broadcasted_iota(jnp.int32, (16, 128), 0) + jnp.where(low, 0, 16)
    start = jnp.zeros_like(token)
    end = jnp.int32(0)
    for k in range(docs_s.shape[1]):
        end = end + docs_s[0, k]
        start = jnp.maximum(start, jnp.where(token >= end, end, 0))
    position = (token - start).astype(F32)
    pair = (lane & 31).astype(F32)
    angle = position * jnp.exp(pair * (-2.0 / ROPE * 9.210340371976184))
    cosine, sine = jnp.cos(angle), jnp.sin(angle)
    front = (lane & 32) == 0
    sine = jnp.where(front, sine, -sine)
    values = latent_v[...].astype(F32)
    inverse = lax.rsqrt(jnp.mean(values * values, axis=1, keepdims=True) + 1e-06)

    def from_z(offset, owner):
        if offset in (1, 7):
            return
        if offset == 3:
            near_sum = zsend[x].astype(F32)
            for slot in p_copies:
                p_copies[slot].wait_recv()
                near_sum = near_sum + precv[slot].astype(F32)
            zsum[...] = near_sum.astype(BF16)
            z_copies[0] = remote(zsum, zrecv.at[x], zs_sem, zr_sem.at[0], z_peer)
            z_copies[0].start()
        z_copies[offset].wait_recv()
        own_a[owner] = own_a[owner] + zrecv[owner].astype(F32)

    x_ring = Ring(x_peer, xsend, xrecv, xs_sem, xr_sem, 5, direct=True)
    mine_a = x_ring.reduce(nx, x, from_z, own_a, True)
    acc_a[...] = x_ring.collect(nx, mine_a)

    for rb in range(2):
        for lb in range(4):
            sum_a[16 * rb : 16 * rb + 16, 128 * lb : 128 * lb + 128] = acc_a[4 * rb + lb]
    scaled = sum_a[...] * gain_v[...]
    dots = jnp.mean(scaled * values, axis=1, keepdims=True)
    kv_row[:, :LATENT] = (inverse * (scaled - values * inverse * inverse * dots)).astype(BF16)
    rope = acc_a[8]
    other = jnp.where(front, pltpu.roll(rope, 96, 1), pltpu.roll(rope, 32, 1))
    rotated = rope * cosine + other * sine
    kv_row[0:16, LATENT:KVW] = rotated[:, :ROPE].astype(BF16)
    kv_row[16:32, LATENT:KVW] = pltpu.roll(rotated, 64, 1)[:, :ROPE].astype(BF16)
    kva[own_rows, :] = dot(kv_row[...], pick_v[...], NN).astype(BF16)

    def block_at(offset, part=None, plane=None):
        head = (zl if plane is None else plane) * nx + (x + offset + nx) % nx
        first, size = (0, ROWS) if part is None else (part * ROWS // 2, ROWS // 2)
        return kva.at[pl.ds(pl.multiple_of(head * ROWS + first, size), size), :]

    g_copies, f_copies = {}, {}

    def along(name, rows, hop):
        g_copies[name] = remote(rows, rows, gs_sem, gr_sem.at[len(g_copies)], x_peer[hop])
        g_copies[name].start()

    def across(name, rows):
        f_copies[name] = remote(rows, rows, fs_sem, fr_sem.at[len(f_copies)], z_peer)
        f_copies[name].start()

    if nx > 1:
        along(2, block_at(0), 2)
        along(-2, block_at(0), -2)
    across(0, block_at(0))
    if nx > 1:
        along(1, block_at(0), 1)
        along(-1, block_at(0), -1)
        f_copies[0].wait_recv()
        along("near", block_at(0, plane=1 - zl), 1)
        along("raen", block_at(0, plane=1 - zl), -1)
        g_copies[2].wait_recv()
        across(-2, block_at(-2))
        along("far", block_at(-2), 1)
        along("first", block_at(-2, 0), 2)
        g_copies[-2].wait_recv()
        across(2, block_at(2))
        along("raf", block_at(2), -1)
        along("second", block_at(2, 1), -2)
        f_copies[-2].wait_recv()
        along("over", block_at(-2, plane=1 - zl), 1)
        f_copies[2].wait_recv()
        along("revo", block_at(2, plane=1 - zl), -1)
        g_copies["first"].wait_recv()
        across(4, block_at(4, 0))
        g_copies["second"].wait_recv()
        across(-4, block_at(4, 1))
        for name in (1, -1, "near", "raen", "far", "raf", "over", "revo"):
            g_copies[name].wait_recv()
        f_copies[4].wait_recv()
        f_copies[-4].wait_recv()
    else:
        f_copies[0].wait_recv()

    product = dot(kva[...], hidden_v[...], TT)
    for k in range(2):
        for j in range(ny):
            at = (k * ny + j) * block
            w_f32[k, j] = product[at : at + block].reshape(w_f32.shape[2:])
    csend[...] = w_f32[1 - core].astype(BF16)
    c_copies = {}
    order = [0] if ny == 1 else [4, 3, 5, 1, 7, 2, 6, 0]
    for d in order:
        to = (y + d) % ny
        c_copies[d] = remote(csend.at[to], crecv.at[to], cs_sem, cr_sem.at[d], core_peer)
        c_copies[d].start()

    own_c = w_f32.at[core]

    def from_core(offset, owner):
        c_copies[offset].wait_recv()
        own_c[owner] = own_c[owner] + crecv[owner].astype(F32)

    y_ring = Ring(y_peer, ysend, yrecv, ys_sem, yr_sem, (block // 8 + 1) // 2)
    mine_c = y_ring.reduce(ny, y, from_core, own_c, False)
    hidden_out[...] = dot(down_p[...], kva[...], NT).astype(BF16)
    total = y_ring.collect(ny, mine_c)
    acc_c[...] = total.reshape(acc_c.shape)
    for k in range(nzh):
        piece = acc_c[k * own : k * own + own, :]
        hi_f32[k, 0:own, :] = piece
        hi_send[k, 0:own, :] = piece.astype(BF16)
    h_copies = {}
    for d in far_first(nzh):
        to = (zh + d) % nzh
        h_copies[d] = remote(hi_send.at[to], hi_recv.at[d], hs_sem, hr_sem.at[d], h_peer[d])
        h_copies[d].start()
    result = hi_f32[zh, 0:own, :]
    for d in far_first(nzh):
        h_copies[d].wait_recv()
        result = result + hi_recv[d, 0:own, :].astype(F32)
    weight_out[...] = result

    def sent(ref, count, sem, recv_sem):
        part = ref.at[pl.ds(0, count)]
        remote(part, part, sem, recv_sem.at[0], z_peer).wait_send()

    sent(zsend, min(nx, 6), zs_sem, zr_sem)
    x_ring.finish(nx)
    if nx > 1:
        sent(zsend, 2, ps_sem, pr_sem)
        sent(kva, 11 * ROWS, gs_sem, gr_sem)
    sent(kva, min(nx, 4) * ROWS, fs_sem, fr_sem)
    remote(csend, crecv, cs_sem, cr_sem.at[0], core_peer).wait_send()
    y_ring.finish(ny)
    if nzh > 1:
        sent(hi_send, nzh - 1, hs_sem, hr_sem)


def on_device(lay, *args):
    key, value, rope, key_lift, value_lift, latent, gain, docs, hidden, down = args
    half = lay.seq // 2
    nx, ny, nzh = lay.nx, lay.ny, lay.nzh
    hidden = hidden.T
    cols = hidden.shape[0]
    rows8 = (lay.block // 8, 8, cols)
    dma = pltpu.SemaphoreType.DMA
    any_spec = pl.BlockSpec(memory_space=pl.ANY)
    scratch = [
        pltpu.VMEM((2, half, key.shape[1]), BF16),
        pltpu.VMEM((2, half, value.shape[1]), BF16),
        pltpu.VMEM((2, half, rope.shape[1]), BF16),
        pltpu.VMEM(key_lift.shape, BF16),
        pltpu.VMEM(value_lift.shape, BF16),
        pltpu.VMEM((ROWS, LATENT), BF16),
        pltpu.VMEM((1, LATENT), F32),
        pltpu.SMEM(docs.shape, jnp.int32),
        pltpu.VMEM(hidden.shape, BF16),
        pltpu.VMEM(down.shape, BF16),
        dma((13,)),
        pltpu.VMEM((rope.shape[1], 128), BF16),
        pltpu.VMEM((KVW, lay.kp), BF16),
        pltpu.VMEM((down.shape[0], lay.kp), BF16),
        pltpu.VMEM((nx, TILES, 16, 128), F32),
        pltpu.VMEM((nx, TILES, 16, 128), BF16),
        pltpu.VMEM((nx, TILES, 16, 128), BF16),
        pltpu.VMEM((2, TILES, 16, 128), BF16),
        pltpu.VMEM((TILES, 16, 128), BF16),
        pltpu.VMEM((7, TILES, 16, 128), BF16),
        pltpu.VMEM((7, TILES, 16, 128), BF16),
        pltpu.VMEM((TILES, 16, 128), F32),
        pltpu.VMEM((ROWS, LATENT), F32),
        pltpu.VMEM((ROWS, KVW), BF16),
        pltpu.VMEM((lay.seq, lay.kp), BF16),
        pltpu.VMEM((2, ny, *rows8), F32),
        pltpu.VMEM((ny, *rows8), BF16),
        pltpu.VMEM((ny, *rows8), BF16),
        pltpu.VMEM((7, *rows8), BF16),
        pltpu.VMEM((7, *rows8), BF16),
        pltpu.VMEM((lay.block, cols), F32),
        pltpu.VMEM((nzh, lay.ownp, cols), F32),
        pltpu.VMEM((nzh, lay.ownp, cols), BF16),
        pltpu.VMEM((nzh, lay.ownp, cols), BF16),
        dma,
        dma((8,)),
        dma,
        dma((2,)),
        dma,
        dma((8,)),
        dma,
        dma((12,)),
        dma,
        dma((5,)),
        dma,
        dma((8,)),
        dma,
        dma((8,)),
        dma,
        dma((nzh,)),
    ]
    hidden_grad, weight_grad = pl.pallas_call(
        functools.partial(kernel, lay),
        out_shape=(
            pltpu.VMEM((cols, lay.seq), BF16),
            pltpu.VMEM((lay.own, cols), F32),
        ),
        in_specs=[any_spec] * 10,
        out_specs=(pl.BlockSpec(memory_space=pltpu.VMEM),) * 2,
        scratch_shapes=scratch,
        compiler_params=pltpu.CompilerParams(
            collective_id=0, has_side_effects=True, vmem_limit_bytes=60 * 1024 * 1024
        ),
        name="latent_backward",
    )(key, value, rope, key_lift, value_lift, latent, gain.reshape(1, -1), docs, hidden, down)
    return hidden_grad.T, weight_grad


def solution(mesh, lay=Layout(4, 8, 8)):
    return jax.shard_map(
        functools.partial(on_device, lay),
        mesh=mesh,
        in_specs=(
            P("group", "head"),
            P("group", "head"),
            P("group", "head"),
            P(None, "head"),
            P(None, "head"),
            P("group", None),
            P(),
            P("group", None),
            P("group", "head"),
            P("head", None),
        ),
        out_specs=(P("group", "head"), P("group", "head")),
        check_vma=False,
    )
```

```python
import functools

import jax
import jax.numpy as jnp
from jax import lax
from jax.experimental import pallas as pl
from jax.experimental.pallas import tpu as pltpu
from jax.sharding import PartitionSpec as P

LATENT = 512
ROPE = 64
KVW = LATENT + ROPE
ROWS = 32
TILES = KVW * ROWS // (16 * 128)
MESH = pl.DeviceIdType.MESH
NT = (((1,), (1,)), ((), ()))
TT = (((0,), (1,)), ((), ()))
NN = (((1,), (0,)), ((), ()))
F32 = jnp.float32
BF16 = jnp.bfloat16


class Layout:
    def __init__(self, nzh, ny, nx):
        self.nzh, self.ny, self.nx = nzh, ny, nx
        self.heads = 2 * nx
        self.groups = 2 * ny * nzh
        self.seq = ROWS * self.heads
        self.own = KVW // self.groups
        self.block = -(-nzh * self.own // 8) * 8
        self.used = 2 * ny * self.block
        self.kp = -(-self.used // 128) * 128
        self.ownp = -(-self.own // 16) * 16


def far_first(n):
    return sorted(range(1, n), key=lambda d: (-min(d, n - d), d))


def remote(src, dst, send, recv, peer):
    return pltpu.make_async_remote_copy(src, dst, send, recv, device_id=peer, device_id_type=MESH)


class Ring:
    PLAN = {"far": (0, 3, 1), "raf": (1, -3, -1), "add": (3, 2, 2), "dda": (4, -2, -2), "one": (5, 1, 1), "eno": (6, -1, -1)}

    def __init__(self, peer, send, recv, send_sem, recv_sem, split, direct=False):
        self.peer, self.send, self.recv, self.split = peer, send, recv, split
        self.direct = direct
        self.send_sem, self.recv_sem = send_sem, recv_sem
        self.copies = {}

    def start(self, name, src, dst, sem, hop):
        self.copies[name] = remote(src, dst, self.send_sem, self.recv_sem.at[sem], self.peer[hop])
        self.copies[name].start()

    def put(self, name, term):
        slot, offset, hop = self.PLAN[name]
        hop = offset if self.direct else hop
        self.send[slot] = term.astype(BF16)
        self.start(name, self.send.at[slot], self.recv.at[slot], slot, hop)

    def put_opposite(self, term):
        self.send[2] = term.astype(BF16)
        first, second = pl.ds(0, self.split), pl.ds(self.split, self.send.shape[1] - self.split)
        self.start("first", self.send.at[2, first], self.recv.at[2, first], 2, 2)
        self.start("second", self.send.at[2, second], self.recv.at[2, second], 7, -2)

    def take(self, name):
        self.copies[name].wait_recv()
        return self.recv[self.PLAN[name][0]].astype(F32)

    def relay(self, name, term_ref, index):
        far, part = ("far", "first") if name == "add" else ("raf", "second")
        if not self.direct:
            self.copies[far].wait_recv()
        self.copies[part].wait_recv()
        rows = pl.ds(0, self.split) if name == "add" else pl.ds(self.split, self.send.shape[1] - self.split)
        if not self.direct:
            term_ref[index] = term_ref[index] + self.recv[self.PLAN[far][0]].astype(F32)
        whole = term_ref.at[index]
        whole[rows] = whole[rows] + self.recv[2, rows].astype(F32)
        self.put(name, term_ref[index])

    def reduce(self, size, me, ready, term_ref, near_left):
        def at(offset):
            return (me + offset + size) % size

        def term(offset):
            ready(offset % size, at(offset))
            return term_ref[at(offset)]

        if size == 1:
            return term(0)
        self.put_opposite(term(4))
        self.put("far", term(3))
        self.put("raf", term(-3))
        if not near_left:
            self.put("one", term(1))
            self.put("eno", term(-1))
        ready(2, at(2))
        ready(6, at(-2))
        self.relay("add", term_ref, at(2))
        self.relay("dda", term_ref, at(-2))
        return term(0)

    def collect(self, size, total):
        if size == 1:
            return total
        for name in ("one", "eno", *(("far", "raf") if self.direct else ()), "add", "dda"):
            total = total + self.take(name)
        return total

    def finish(self, size):
        if size > 1:
            remote(self.send, self.recv, self.send_sem, self.recv_sem.at[0], self.peer[1]).wait_send()


def dot(a, b, dims):
    return lax.dot_general(a, b, dims, preferred_element_type=F32)


def kernel(
    lay,
    key_hbm,
    value_hbm,
    rope_hbm,
    key_lift_hbm,
    value_lift_hbm,
    latent_hbm,
    gain_hbm,
    docs_hbm,
    hidden_hbm,
    down_hbm,
    hidden_out,
    weight_out,
    key_v,
    value_v,
    rope_v,
    key_lift_v,
    value_lift_v,
    latent_v,
    gain_v,
    docs_s,
    hidden_v,
    down_v,
    load_sem,
    fold_v,
    pick_v,
    down_p,
    own_a,
    zsend,
    zrecv,
    precv,
    zsum,
    xsend,
    xrecv,
    acc_a,
    sum_a,
    kv_row,
    kva,
    w_f32,
    csend,
    crecv,
    ysend,
    yrecv,
    acc_c,
    hi_f32,
    hi_send,
    hi_recv,
    zs_sem,
    zr_sem,
    ps_sem,
    pr_sem,
    xs_sem,
    xr_sem,
    gs_sem,
    gr_sem,
    fs_sem,
    fr_sem,
    cs_sem,
    cr_sem,
    ys_sem,
    yr_sem,
    hs_sem,
    hr_sem,
):
    nx, ny, nzh = lay.nx, lay.ny, lay.nzh
    half = lay.seq // 2
    g = lax.axis_index("group")
    h = lax.axis_index("head")
    core, y, zh = g % 2, (g // 2) % ny, g // (2 * ny)
    x, zl = h % nx, h // nx

    z_peer = (g, (1 - zl) * nx + x)
    core_peer = (g + 1 - 2 * core, h)
    near = (2, -2, 1, -1)
    x_peer = {d: (g, zl * nx + (x + d + nx) % nx) for d in (3, -3, *near) if nx > 1}
    y_peer = {d: ((zh * ny + (y + d + ny) % ny) * 2 + core, h) for d in near if ny > 1}
    h_peer = {d: ((((zh + d) % nzh) * ny + y) * 2 + core, h) for d in range(1, nzh)}
    peers = [z_peer, core_peer, *x_peer.values(), *y_peer.values(), *h_peer.values()]

    theirs = pl.ds(pl.multiple_of((1 - zl) * half, half), half)
    mine = pl.ds(pl.multiple_of(zl * half, half), half)
    own_rows = pl.ds(pl.multiple_of(h * ROWS, ROWS), ROWS)
    loads = []

    def load(src, dst):
        copy = pltpu.make_async_copy(src, dst, load_sem.at[len(loads)])
        copy.start()
        loads.append(copy)
        return copy

    first = [load(key_lift_hbm, key_lift_v), load(key_hbm.at[theirs, :], key_v.at[0])]
    second = [
        load(value_lift_hbm, value_lift_v),
        load(value_hbm.at[theirs, :], value_v.at[0]),
        load(rope_hbm.at[theirs, :], rope_v.at[0]),
    ]

    barrier = pltpu.get_barrier_semaphore()
    for peer in peers:
        pl.semaphore_signal(barrier, inc=1, device_id=peer, device_id_type=MESH)

    width = rope_v.shape[2]
    fold_row = lax.broadcasted_iota(jnp.int32, (width, 128), 0)
    fold_col = lax.broadcasted_iota(jnp.int32, (width, 128), 1)
    fold_v[...] = jnp.where((fold_row & 63) == (fold_col & 63), 1.0, 0.0).astype(BF16)
    low = lax.broadcasted_iota(jnp.int32, (16, 128), 1) < 64

    def tiles(terms, ropes, chunk):
        base = chunk * ROWS
        for block in range(2):
            rows = slice(base + 16 * block, base + 16 * block + 16)
            for lane in range(4):
                yield 4 * block + lane, terms[rows, 128 * lane : 128 * lane + 128]
        yield 8, jnp.where(low, ropes[base : base + 16], ropes[base + 16 : base + 32])

    for copy in first:
        copy.wait()
    terms = dot(key_v[0], key_lift_v[...], NT)
    for copy in second:
        copy.wait()
    third = [
        load(key_hbm.at[mine, :], key_v.at[1]),
        load(value_hbm.at[mine, :], value_v.at[1]),
        load(rope_hbm.at[mine, :], rope_v.at[1]),
    ]
    fourth = [
        load(down_hbm, down_v),
        load(latent_hbm.at[own_rows, :], latent_v),
        load(gain_hbm, gain_v),
        load(docs_hbm, docs_s),
        load(hidden_hbm, hidden_v),
    ]
    terms = terms + dot(value_v[0], value_lift_v[...], NT)
    ropes = dot(rope_v[0], fold_v[...], NN)
    for chunk in range(nx):
        for i, tile in tiles(terms, ropes, chunk):
            zsend[chunk, i] = tile.astype(BF16)
    pl.semaphore_wait(barrier, len(peers))

    order = [0] if nx == 1 else [4, 3, 5, 2, 6]
    z_copies, p_copies = {}, {}
    for d in order:
        to = (x + d) % nx
        z_copies[d] = remote(zsend.at[to], zrecv.at[to], zs_sem, zr_sem.at[d], z_peer)
        z_copies[d].start()
        if d == 4:
            for slot, hop in enumerate((1, -1)):
                to = (x + hop + nx) % nx
                p_copies[slot] = remote(zsend.at[to], precv.at[slot], ps_sem, pr_sem.at[slot], x_peer[hop])
                p_copies[slot].start()
    for copy in third:
        copy.wait()
    terms = dot(key_v[1], key_lift_v[...], NT) + dot(value_v[1], value_lift_v[...], NT)
    ropes = dot(rope_v[1], fold_v[...], NN)
    for chunk in range(nx):
        for i, tile in tiles(terms, ropes, chunk):
            own_a[chunk, i] = tile

    def from_z(offset, owner):
        if offset == 3:
            near_sum = zsend[x].astype(F32)
            for slot in p_copies:
                p_copies[slot].wait_recv()
                near_sum = near_sum + precv[slot].astype(F32)
            zsum[...] = near_sum.astype(BF16)
            z_copies[0] = remote(zsum, zrecv.at[x], zs_sem, zr_sem.at[0], z_peer)
            z_copies[0].start()
        z_copies[offset].wait_recv()
        own_a[owner] = own_a[owner] + zrecv[owner].astype(F32)

    x_ring = Ring(x_peer, xsend, xrecv, xs_sem, xr_sem, 5, direct=True)
    if nx > 1:
        x_ring.put("one", own_a[(x + 1) % nx])
        x_ring.put("eno", own_a[(x + nx - 1) % nx])

    for copy in fourth:
        copy.wait()
    block, own = lay.block, lay.own
    col = lax.broadcasted_iota(jnp.int32, (KVW, lay.kp), 1)
    row = lax.broadcasted_iota(jnp.int32, (KVW, lay.kp), 0)
    chunk_of = jnp.zeros_like(col)
    for k in range(1, 2 * ny):
        chunk_of = chunk_of + jnp.where(col >= k * block, 1, 0)
    q = col - chunk_of * block
    hi_of = jnp.zeros_like(col)
    for k in range(1, nzh):
        hi_of = hi_of + jnp.where(q >= k * own, 1, 0)
    core_of = jnp.where(chunk_of >= ny, 1, 0)
    source = ((hi_of * ny + chunk_of - core_of * ny) * 2 + core_of) * own + q - hi_of * own
    picked = (row == source) & (q < nzh * own) & (col < lay.used)
    pick_v[...] = jnp.where(picked, 1.0, 0.0).astype(BF16)
    down_p[...] = dot(down_v[...], pick_v[...], NN).astype(BF16)

    lane = lax.broadcasted_iota(jnp.int32, (16, 128), 1)
    token = h * ROWS + lax.broadcasted_iota(jnp.int32, (16, 128), 0) + jnp.where(low, 0, 16)
    start = jnp.zeros_like(token)
    end = jnp.int32(0)
    for k in range(docs_s.shape[1]):
        end = end + docs_s[0, k]
        start = jnp.maximum(start, jnp.where(token >= end, end, 0))
    position = (token - start).astype(F32)
    pair = (lane & 31).astype(F32)
    angle = position * jnp.exp(pair * (-2.0 / ROPE * 9.210340371976184))
    cosine, sine = jnp.cos(angle), jnp.sin(angle)
    front = (lane & 32) == 0
    sine = jnp.where(front, sine, -sine)
    values = latent_v[...].astype(F32)
    inverse = lax.rsqrt(jnp.mean(values * values, axis=1, keepdims=True) + 1e-06)

    mine_a = x_ring.reduce(nx, x, from_z, own_a, True)
    acc_a[...] = x_ring.collect(nx, mine_a)

    for rb in range(2):
        for lb in range(4):
            sum_a[16 * rb : 16 * rb + 16, 128 * lb : 128 * lb + 128] = acc_a[4 * rb + lb]
    scaled = sum_a[...] * gain_v[...]
    dots = jnp.mean(scaled * values, axis=1, keepdims=True)
    kv_row[:, :LATENT] = (inverse * (scaled - values * inverse * inverse * dots)).astype(BF16)
    rope = acc_a[8]
    other = jnp.where(front, pltpu.roll(rope, 96, 1), pltpu.roll(rope, 32, 1))
    rotated = rope * cosine + other * sine
    kv_row[0:16, LATENT:KVW] = rotated[:, :ROPE].astype(BF16)
    kv_row[16:32, LATENT:KVW] = pltpu.roll(rotated, 64, 1)[:, :ROPE].astype(BF16)
    kva[own_rows, :] = dot(kv_row[...], pick_v[...], NN).astype(BF16)

    def block_at(offset, part=None, plane=None):
        head = (zl if plane is None else plane) * nx + (x + offset + nx) % nx
        first, size = (0, ROWS) if part is None else (part * ROWS // 2, ROWS // 2)
        return kva.at[pl.ds(pl.multiple_of(head * ROWS + first, size), size), :]

    def keep_product(product, add=False):
        for k in range(2):
            for j in range(ny):
                at = (k * ny + j) * block
                piece = product[at : at + block].reshape(w_f32.shape[2:])
                w_f32[k, j] = w_f32[k, j] + piece if add else piece

    g_copies, f_copies = {}, {}

    def along(name, rows, hop):
        g_copies[name] = remote(rows, rows, gs_sem, gr_sem.at[len(g_copies)], x_peer[hop])
        g_copies[name].start()

    def across(name, rows):
        f_copies[name] = remote(rows, rows, fs_sem, fr_sem.at[len(f_copies)], z_peer)
        f_copies[name].start()

    if nx > 1:
        along(2, block_at(0), 2)
        along(-2, block_at(0), -2)
    across(0, block_at(0))
    if nx > 1:
        along(1, block_at(0), 1)
        along(-1, block_at(0), -1)
        f_copies[0].wait_recv()
        along("near", block_at(0, plane=1 - zl), 1)
        along("raen", block_at(0, plane=1 - zl), -1)
        g_copies[2].wait_recv()
        across(-2, block_at(-2))
        along("far", block_at(-2), 1)
        along("first", block_at(-2, 0), 2)
        g_copies[-2].wait_recv()
        across(2, block_at(2))
        along("raf", block_at(2), -1)
        along("second", block_at(2, 1), -2)
        f_copies[-2].wait_recv()
        along("over", block_at(-2, plane=1 - zl), 1)
        f_copies[2].wait_recv()
        along("revo", block_at(2, plane=1 - zl), -1)
        g_copies["first"].wait_recv()
        across(4, block_at(4, 0))
        g_copies["second"].wait_recv()
        across(-4, block_at(4, 1))
        for name in (1, -1, "far", "raf"):
            g_copies[name].wait_recv()
        keep_product(dot(kva[mine, :], hidden_v[:, mine], TT))
        for name in ("near", "raen", "over", "revo"):
            g_copies[name].wait_recv()
        f_copies[4].wait_recv()
        f_copies[-4].wait_recv()
    else:
        keep_product(dot(kva[mine, :], hidden_v[:, mine], TT))
        f_copies[0].wait_recv()

    keep_product(dot(kva[theirs, :], hidden_v[:, theirs], TT), add=True)
    csend[...] = w_f32[1 - core].astype(BF16)
    c_copies = {}
    order = [0] if ny == 1 else [4, 3, 5, 1, 7, 2, 6, 0]
    for d in order:
        to = (y + d) % ny
        c_copies[d] = remote(csend.at[to], crecv.at[to], cs_sem, cr_sem.at[d], core_peer)
        c_copies[d].start()

    own_c = w_f32.at[core]

    def from_core(offset, owner):
        c_copies[offset].wait_recv()
        own_c[owner] = own_c[owner] + crecv[owner].astype(F32)

    y_ring = Ring(y_peer, ysend, yrecv, ys_sem, yr_sem, (block // 8 + 1) // 2)
    mine_c = y_ring.reduce(ny, y, from_core, own_c, False)
    hidden_out[...] = dot(down_p[...], kva[...], NT).astype(BF16)
    total = y_ring.collect(ny, mine_c)
    acc_c[...] = total.reshape(acc_c.shape)
    for k in range(nzh):
        piece = acc_c[k * own : k * own + own, :]
        hi_f32[k, 0:own, :] = piece
        hi_send[k, 0:own, :] = piece.astype(BF16)
    h_copies = {}
    for d in far_first(nzh):
        to = (zh + d) % nzh
        h_copies[d] = remote(hi_send.at[to], hi_recv.at[d], hs_sem, hr_sem.at[d], h_peer[d])
        h_copies[d].start()
    result = hi_f32[zh, 0:own, :]
    for d in far_first(nzh):
        h_copies[d].wait_recv()
        result = result + hi_recv[d, 0:own, :].astype(F32)
    weight_out[...] = result

    def sent(ref, count, sem, recv_sem):
        part = ref.at[pl.ds(0, count)]
        remote(part, part, sem, recv_sem.at[0], z_peer).wait_send()

    sent(zsend, min(nx, 6), zs_sem, zr_sem)
    x_ring.finish(nx)
    if nx > 1:
        sent(zsend, 2, ps_sem, pr_sem)
        sent(kva, 11 * ROWS, gs_sem, gr_sem)
    sent(kva, min(nx, 4) * ROWS, fs_sem, fr_sem)
    remote(csend, crecv, cs_sem, cr_sem.at[0], core_peer).wait_send()
    y_ring.finish(ny)
    if nzh > 1:
        sent(hi_send, nzh - 1, hs_sem, hr_sem)


def hand_over(hidden_ref, weight_ref, hidden_out, weight_out, sem):
    copies = [
        pltpu.make_async_copy(hidden_ref, hidden_out, sem.at[0]),
        pltpu.make_async_copy(weight_ref, weight_out, sem.at[1]),
    ]
    for copy in copies:
        copy.start()
    for copy in copies:
        copy.wait()


def on_device(lay, *args):
    key, value, rope, key_lift, value_lift, latent, gain, docs, hidden, down = args
    half = lay.seq // 2
    nx, ny, nzh = lay.nx, lay.ny, lay.nzh
    hidden = hidden.T
    cols = hidden.shape[0]
    rows8 = (lay.block // 8, 8, cols)
    dma = pltpu.SemaphoreType.DMA
    any_spec = pl.BlockSpec(memory_space=pl.ANY)
    scratch = [
        pltpu.VMEM((2, half, key.shape[1]), BF16),
        pltpu.VMEM((2, half, value.shape[1]), BF16),
        pltpu.VMEM((2, half, rope.shape[1]), BF16),
        pltpu.VMEM(key_lift.shape, BF16),
        pltpu.VMEM(value_lift.shape, BF16),
        pltpu.VMEM((ROWS, LATENT), BF16),
        pltpu.VMEM((1, LATENT), F32),
        pltpu.SMEM(docs.shape, jnp.int32),
        pltpu.VMEM(hidden.shape, BF16),
        pltpu.VMEM(down.shape, BF16),
        dma((13,)),
        pltpu.VMEM((rope.shape[1], 128), BF16),
        pltpu.VMEM((KVW, lay.kp), BF16),
        pltpu.VMEM((down.shape[0], lay.kp), BF16),
        pltpu.VMEM((nx, TILES, 16, 128), F32),
        pltpu.VMEM((nx, TILES, 16, 128), BF16),
        pltpu.VMEM((nx, TILES, 16, 128), BF16),
        pltpu.VMEM((2, TILES, 16, 128), BF16),
        pltpu.VMEM((TILES, 16, 128), BF16),
        pltpu.VMEM((7, TILES, 16, 128), BF16),
        pltpu.VMEM((7, TILES, 16, 128), BF16),
        pltpu.VMEM((TILES, 16, 128), F32),
        pltpu.VMEM((ROWS, LATENT), F32),
        pltpu.VMEM((ROWS, KVW), BF16),
        pltpu.VMEM((lay.seq, lay.kp), BF16),
        pltpu.VMEM((2, ny, *rows8), F32),
        pltpu.VMEM((ny, *rows8), BF16),
        pltpu.VMEM((ny, *rows8), BF16),
        pltpu.VMEM((7, *rows8), BF16),
        pltpu.VMEM((7, *rows8), BF16),
        pltpu.VMEM((lay.block, cols), F32),
        pltpu.VMEM((nzh, lay.ownp, cols), F32),
        pltpu.VMEM((nzh, lay.ownp, cols), BF16),
        pltpu.VMEM((nzh, lay.ownp, cols), BF16),
        dma,
        dma((8,)),
        dma,
        dma((2,)),
        dma,
        dma((8,)),
        dma,
        dma((12,)),
        dma,
        dma((5,)),
        dma,
        dma((8,)),
        dma,
        dma((8,)),
        dma,
        dma((nzh,)),
    ]
    hidden_grad, weight_grad = pl.pallas_call(
        functools.partial(kernel, lay),
        out_shape=(
            pltpu.VMEM((cols, lay.seq), BF16),
            pltpu.VMEM((lay.own, cols), F32),
        ),
        in_specs=[any_spec] * 10,
        out_specs=(pl.BlockSpec(memory_space=pltpu.VMEM),) * 2,
        scratch_shapes=scratch,
        compiler_params=pltpu.CompilerParams(
            collective_id=0, has_side_effects=True, vmem_limit_bytes=60 * 1024 * 1024
        ),
        name="latent_backward",
    )(key, value, rope, key_lift, value_lift, latent, gain.reshape(1, -1), docs, hidden, down)
    hidden_grad, weight_grad = pl.pallas_call(
        hand_over,
        out_shape=(
            jax.ShapeDtypeStruct((cols, lay.seq), BF16),
            jax.ShapeDtypeStruct((lay.own, cols), F32),
        ),
        in_specs=[any_spec] * 2,
        out_specs=(any_spec,) * 2,
        scratch_shapes=[dma((2,))],
        compiler_params=pltpu.CompilerParams(vmem_limit_bytes=4 * 1024 * 1024),
        name="hand_over",
    )(hidden_grad, weight_grad)
    return hidden_grad.T, weight_grad


def solution(mesh, lay=Layout(4, 8, 8)):
    return jax.shard_map(
        functools.partial(on_device, lay),
        mesh=mesh,
        in_specs=(
            P("group", "head"),
            P("group", "head"),
            P("group", "head"),
            P(None, "head"),
            P(None, "head"),
            P("group", None),
            P(),
            P("group", None),
            P("group", "head"),
            P("head", None),
        ),
        out_specs=(P("group", "head"), P("group", "head")),
        check_vma=False,
    )
```
